256 devices in a mesh: seq: 32 (over z, y), uly: 8 (over x, core).
Axes of the slice: x: 4, y: 4, z: 8, core: 2. Of those that a mesh axis runs over, the one named last changes fastest.
Arguments:
- queries: bfloat16 [32768, 5120], P(('seq', 'uly')), may hold values from -27 to 27
- keys: bfloat16 [32768, 5120], P(('seq', 'uly')), may hold values from -9 to 9
- values: bfloat16 [32768, 5120], P(('seq', 'uly')), may hold values from -6 to 6
- block_lists: int32 [256, 12], P('seq'), may hold values from 0 to 255, as said below
- block_counts: int32 [256], P('seq'), may hold values from 4 to 12
Outputs:
- attended: bfloat16 [32768, 5120], P(('seq', 'uly'))
The draws below stay inside these ranges and needn't reach their ends.
Inputs may be any that keep to these rules, and one draw needn't show every extreme that they name: `block_lists`: each row names 12 different blocks, its first entry being the query block itself; only the first block_counts entries of a row are used, the rest are block numbers too. Over the used entries of the 8 query blocks of one group (blocks g * 8 to (g + 1) * 8 - 1), at most 2 different blocks of any other group are named, and in every group exactly 2 of some other group.
All inputs are finite; a program needn't handle non-finite values.
Results may differ from the reference program's by a relative error of at most 0.003.
Values may be sent and summed in bfloat16 or wider, within the bound.
A program may use at most 128 MiB of HBM per device.

```python
import jax
import jax.numpy as jnp
from jax import lax

NUM_HEADS = 40
HEAD_DIM = 128
BLOCK_LEN = 128
LIST_LEN = 12
PEER_SLOTS = 2
MODEL_WIDTH = 5120
TOKENS = 32768
GROUP_BLOCKS = 8
QBLOCKS = 256


def attention_inputs(key):
    base = jax.random.fold_in(key, 5)
    first, second = jax.random.split(base, 2)
    shape = (TOKENS, MODEL_WIDTH)
    query_part = jax.random.truncated_normal(first, -4.0, 4.0, shape) * 1.6
    key_part = jax.random.truncated_normal(second, -4.0, 4.0, shape) * 1.6
    return (query_part, key_part)


def draw_queries(key, part):
    return attention_inputs(key)[0].astype(jnp.bfloat16)


def draw_keys(key, part):
    return attention_inputs(key)[1].astype(jnp.bfloat16)


def mask_tables(key):
    base = jax.random.fold_in(key, 11)
    first, second, third, fourth = jax.random.split(base, 4)
    groups = QBLOCKS // GROUP_BLOCKS
    per_group = GROUP_BLOCKS
    order = jax.random.randint(first, (groups, groups, per_group), 0, 1 << 20) * per_group + jnp.arange(per_group, dtype=jnp.int32)
    picked = lax.top_k(order, PEER_SLOTS)[1].astype(jnp.int32)
    group_ids = jnp.arange(groups, dtype=jnp.int32)
    local_cands = group_ids[:, None] * per_group + jnp.arange(per_group, dtype=jnp.int32)[None, :]
    remote_cands = (group_ids[None, :, None] * per_group + picked).reshape(groups, groups * PEER_SLOTS)
    cands = jnp.concatenate([local_cands, remote_cands], axis=1)
    cand_width = per_group + groups * PEER_SLOTS
    block_ids = jnp.arange(QBLOCKS, dtype=jnp.int32)
    home_group = block_ids // per_group
    home_index = block_ids % per_group
    cand_index = jnp.arange(cand_width, dtype=jnp.int32)
    is_remote = cand_index[None, :] >= per_group
    cand_group = jnp.where(is_remote, (cand_index[None, :] - per_group) // PEER_SLOTS, home_group[:, None])
    score = jax.random.randint(second, (QBLOCKS, cand_width), 0, 1 << 20) * cand_width + cand_index[None, :]
    same_group = is_remote & (cand_group == home_group[:, None])
    own_block = (cand_index[None, :] == home_index[:, None]) & jnp.logical_not(is_remote)
    neighbour = (cand_index[None, :] == home_index[:, None] - 1) & (home_index[:, None] > 0) & jnp.logical_not(is_remote)
    next_group = is_remote & (cand_group == (home_group[:, None] + 1) % groups) & (home_index[:, None] == 0)
    score = score + jnp.where(own_block, 1 << 29, 0) + jnp.where(neighbour | next_group, 1 << 28, 0)
    score = jnp.where(same_group, cand_index[None, :] - cand_width, score)
    chosen = lax.top_k(score, LIST_LEN)[1].astype(jnp.int32)
    lists = jnp.take_along_axis(cands[home_group], chosen, axis=1).astype(jnp.int32)
    spread = jax.random.randint(third, (groups,), 6, LIST_LEN + 1)
    raw = jax.random.randint(fourth, (QBLOCKS,), 0, 1 << 20)
    counts = raw % (spread[home_group] - 3) + 4
    counts = jnp.where(block_ids == 0, LIST_LEN, jnp.where(block_ids == 1, 4, counts))
    return (lists, counts.astype(jnp.int32))


def draw_block_lists(key, part):
    return mask_tables(key)[0]


def draw_block_counts(key, part):
    return mask_tables(key)[1]


def shard_levels(rng, dims, cuts, low, largest):
    level = 1.0
    for dim, shards_of in cuts:
        steps = jax.random.uniform(jax.random.fold_in(jax.random.fold_in(rng, 6), dim), (shards_of,), jnp.float32, low / len(cuts), largest / len(cuts))
        level = level * jnp.repeat(jnp.exp(steps), dims[dim] // shards_of).reshape((-1,) + (1,) * (len(dims) - 1 - dim))
    return level


def noise(stream_key, dims, scale, limit, shards=(), held_as=jnp.bfloat16):
    values = scale * jax.random.normal(stream_key, dims, jnp.float32)
    if shards:
        values = values * shard_levels(stream_key, dims, shards, -0.22, 0.18)
    return jnp.clip(values, -limit, limit).astype(held_as)


def setup_inputs(seed: int = 0) -> dict:
    arg_keys = jax.random.split(jax.random.key(seed), 6)
    queries = draw_queries(jax.random.fold_in(arg_keys[5], 71), 0)
    keys = draw_keys(jax.random.fold_in(arg_keys[5], 71), 0)
    values = noise(arg_keys[2], (TOKENS, MODEL_WIDTH), 1.0, 6.0, ((0, 256),))
    block_lists = draw_block_lists(jax.random.fold_in(arg_keys[5], 71), 0)
    block_counts = draw_block_counts(jax.random.fold_in(arg_keys[5], 71), 0)
    return {"queries": queries, "keys": keys, "values": values, "block_lists": block_lists, "block_counts": block_counts}


def reference(queries, keys, values, block_lists, block_counts):
    token_count, feature_width = queries.shape
    query_blocks = queries.reshape(QBLOCKS, BLOCK_LEN, NUM_HEADS, HEAD_DIM)
    key_blocks = keys.reshape(QBLOCKS, BLOCK_LEN, NUM_HEADS, HEAD_DIM)
    value_blocks = values.reshape(QBLOCKS, BLOCK_LEN, NUM_HEADS, HEAD_DIM)
    score_scale = HEAD_DIM ** -0.5

    def attend(inputs):
        q_block, named_blocks, block_count = inputs
        key_part = jnp.take(key_blocks, named_blocks, axis=0).reshape(LIST_LEN * BLOCK_LEN, NUM_HEADS, HEAD_DIM)
        value_part = jnp.take(value_blocks, named_blocks, axis=0).reshape(LIST_LEN * BLOCK_LEN, NUM_HEADS, HEAD_DIM)
        scores = jnp.einsum("qhd,khd->hqk", q_block.astype(jnp.float32), key_part.astype(jnp.float32)) * score_scale
        live_keys = jnp.repeat(jnp.arange(LIST_LEN, dtype=jnp.int32) < block_count, BLOCK_LEN)
        scores = jnp.where(live_keys[None, None, :], scores, -jnp.inf)
        row_max = jnp.max(scores, axis=2, keepdims=True)
        weights = jnp.exp(scores - row_max)
        weight_sum = jnp.sum(weights, axis=2)
        rounded = lax.optimization_barrier(weights.astype(jnp.bfloat16)).astype(jnp.float32)
        blended = jnp.einsum("hqk,khd->qhd", rounded, value_part.astype(jnp.float32))
        result = blended / jnp.transpose(weight_sum)[:, :, None]
        return result.astype(jnp.bfloat16).reshape(BLOCK_LEN, NUM_HEADS * HEAD_DIM)

    attended = lax.map(attend, (query_blocks, block_lists, block_counts))
    return attended.reshape(token_count, feature_width)
```

```python
import jax
import jax.numpy as jnp
from jax import lax
from jax.experimental import pallas as pl
from jax.experimental.pallas import tpu as pltpu
from jax.sharding import PartitionSpec as P

NZ, NY, NX, NC = 8, 4, 4, 2
HD = 128
BL = 128
LIST_LEN = 12
NBLOCKS = NZ * NY * NX * NC
PLANE_HEADS = NX + 1
MESH = pl.DeviceIdType.MESH
EXP2_SCALE = HD ** (-0.5) * 1.4426950408889634
ORDER = (0, 1, 7, 2, 6, 3, 5, 4)
SLOT_B_LANE = 16
COUNT_LANE = 32


def rem(a, n):
    return lax.rem(a, jnp.int32(n))


def div(a, n):
    return lax.div(a, jnp.int32(n))


def kernel(q_ref, k_ref, v_ref, meta_ref, out_ref, kv, qv, ov, meta_v, meta_s, s_ref, l_kv, l_q, l_m, l_o, l_s,
           s_1, s_m, s_a, s_b, s_o, r_a1, r_b1, r_q, r_m, r_o, r_ay, r_ay2, r_as, r_by, r_by2, r_bs, r_bx, r_bxh, r_bx2):
    s = lax.axis_index("seq")
    u = lax.axis_index("uly")
    z, y = div(s, NY), rem(s, NY)
    x, c = div(u, NC), rem(u, NC)

    def dev(z2, y2, x2, c2):
        return (z2 * NY + y2, x2 * NC + c2)

    yp, ym = rem(y + 1, NY), rem(y + NY - 1, NY)
    y2 = rem(y + 2, NY)
    xp, xm = rem(x + 1, NX), rem(x + NX - 1, NX)
    x2 = rem(x + 2, NX)
    sib = dev(z, y, x, 1 - c)
    y_plus, y_minus = dev(z, yp, x, c), dev(z, ym, x, c)
    x_plus, x_minus = dev(z, y, xp, c), dev(z, y, xm, c)

    def slot_a(zz, yy, xx, cc):
        return ((yy * NC + cc) * NZ + zz) * NX + xx

    def base_b(xx, cc, yy):
        return NBLOCKS + ((xx * NC + cc) * NY + yy) * NZ

    def cols(h):
        return pl.ds(pl.multiple_of(h * HD, HD), HD)

    def wait(ref, sem):
        pltpu.make_async_copy(ref, ref, sem).wait()

    def local(src, dst, sem):
        pltpu.make_async_copy(src, dst, sem).start()

    def remote(src, dst, send, recv, target):
        pltpu.make_async_remote_copy(
            src_ref=src, dst_ref=dst, send_sem=send, recv_sem=recv, device_id=target, device_id_type=MESH
        ).start()

    me_a = slot_a(z, y, x, c)
    me_b = base_b(x, c, y) + z
    head_a, head_b = PLANE_HEADS * z + x, PLANE_HEADS * z + NX
    local(meta_ref, meta_v.at[z], l_m)
    local(k_ref.at[:, cols(head_b)], kv.at[me_b, 0], l_kv.at[1])
    local(v_ref.at[:, cols(head_b)], kv.at[me_b, 1], l_kv.at[1])
    local(k_ref.at[:, cols(head_a)], kv.at[me_a, 0], l_kv.at[0])
    local(v_ref.at[:, cols(head_a)], kv.at[me_a, 1], l_kv.at[0])
    local(q_ref.at[:, cols(head_a)], qv.at[z * NX + x], l_q)
    local(q_ref.at[:, cols(head_b)], qv.at[NZ * NX + z], l_q)

    barrier = pltpu.get_barrier_semaphore()

    def greet(i, carry):
        zz, xx = rem(z + div(i, NX), NZ), rem(x + rem(i, NX), NX)
        pl.semaphore_signal(barrier, inc=1, device_id=dev(zz, y, xx, c), device_id_type=MESH)
        return carry

    lax.fori_loop(1, NZ * NX, greet, 0)
    for target in (sib, y_plus, y_minus):
        pl.semaphore_signal(barrier, inc=1, device_id=target, device_id_type=MESH)
    pl.semaphore_wait(barrier, NZ * NX - 1 + 3)

    def step_to(j):
        half = div(j + 1, 2)
        return jnp.where(rem(j, 2) == 1, half, NZ - half)

    def send_meta_b(j, carry):
        t = step_to(j)
        zz = rem(z + t, NZ)
        target = dev(zz, y, x, c)
        h = PLANE_HEADS * zz + NX
        remote(meta_ref, meta_v.at[z], s_m, r_m, target)
        remote(k_ref.at[:, cols(h)], kv.at[me_b, 0], s_1, r_b1, target)
        remote(v_ref.at[:, cols(h)], kv.at[me_b, 1], s_1, r_b1, target)
        return carry

    lax.fori_loop(1, NZ, send_meta_b, 0)

    def send_a(i, carry):
        j = div(i, NX)
        t = jnp.where(j == 0, 0, step_to(j))
        zz, xx = rem(z + t, NZ), rem(x + rem(i, NX), NX)
        target = dev(zz, y, xx, c)
        h = PLANE_HEADS * zz + xx
        o = rem(NZ - t, NZ)
        remote(k_ref.at[:, cols(h)], kv.at[me_a, 0], s_1, r_a1.at[o], target)
        remote(v_ref.at[:, cols(h)], kv.at[me_a, 1], s_1, r_a1.at[o], target)
        return carry

    lax.fori_loop(1, NZ * NX, send_a, 0)

    def send_q(i, carry):
        j = div(i, NX)
        t = jnp.where(j == 0, 0, step_to(j))
        zz, xx = rem(z + t, NZ), rem(x + rem(i, NX), NX)
        remote(q_ref.at[:, cols(PLANE_HEADS * zz + xx)], qv.at[z * NX + x], s_1, r_q, dev(zz, y, xx, c))
        return carry

    lax.fori_loop(1, NZ * NX, send_q, 0)

    def send_qb(j, carry):
        zz = rem(z + step_to(j), NZ)
        remote(q_ref.at[:, cols(PLANE_HEADS * zz + NX)], qv.at[NZ * NX + z], s_1, r_q, dev(zz, y, x, c))
        return carry

    lax.fori_loop(1, NZ, send_qb, 0)

    sent = {"a": 0, "b": 0}

    def push(which, start, n, recv, target):
        part = kv.at[pl.ds(start, n)]
        sent[which] += n
        remote(part, part, s_a if which == "a" else s_b, recv, target)

    def a_own(o):
        base = slot_a(rem(z + o, NZ), y, 0, c)
        if o == 0:
            wait(kv.at[pl.ds(base, NX - 1)], r_a1.at[0])
            wait(kv.at[me_a], l_kv.at[0])
        else:
            wait(kv.at[pl.ds(base, NX)], r_a1.at[o])
        push("a", base, NX, r_ay.at[0, o], y_plus)
        push("a", base, NX, r_ay.at[1, o], y_minus)
        push("a", base, NX, r_as, sib)

    def a_from(side, o):
        base = slot_a(rem(z + o, NZ), ym if side == 0 else yp, 0, c)
        wait(kv.at[pl.ds(base, NX)], r_ay.at[side, o])
        if (o < NZ // 2) == (side == 0):
            push("a", base, NX, r_ay2.at[o], y_plus if side == 0 else y_minus)
        push("a", base, NX, r_as, sib)

    def a_far(o):
        base = slot_a(rem(z + o, NZ), y2, 0, c)
        wait(kv.at[pl.ds(base, NX)], r_ay2.at[o])
        push("a", base, NX, r_as, sib)

    half_z = NZ // 2
    b_rows = (y, ym, yp)

    def b_spread(row, start, n, sems):
        push("b", start, n, sems[0], x_plus)
        push("b", start, n, sems[1], x_minus)
        push("b", start, n, r_bs, sib)

    def b_own():
        base = base_b(x, c, y)
        wait(kv.at[pl.ds(base, NZ - 1)], r_b1)
        wait(kv.at[me_b], l_kv.at[1])
        push("b", base, NZ, r_by.at[0], y_plus)
        push("b", base, NZ, r_by.at[1], y_minus)
        b_spread(0, base, NZ, (r_bx.at[0, 0], r_bx.at[1, 0]))

    def b_from(side):
        base = base_b(x, c, ym if side == 0 else yp)
        wait(kv.at[pl.ds(base, NZ)], r_by.at[side])
        if side == 0:
            push("b", base, half_z, r_by2.at[0], y_plus)
        else:
            push("b", base + half_z, half_z, r_by2.at[1], y_minus)
        b_spread(1 + side, base, NZ, (r_bx.at[0, 1 + side], r_bx.at[1, 1 + side]))

    def b_far(part):
        base = base_b(x, c, y2) + part * half_z
        wait(kv.at[pl.ds(base, half_z)], r_by2.at[part])
        b_spread(3, base, half_z, (r_bxh.at[0, part], r_bxh.at[1, part]))

    def bx_from(side, row):
        base = base_b(xm if side == 0 else xp, c, b_rows[row])
        wait(kv.at[pl.ds(base, NZ)], r_bx.at[side, row])
        part = base + side * half_z
        push("b", part, half_z, r_bx2.at[side, row], x_plus if side == 0 else x_minus)
        push("b", base, NZ, r_bs, sib)

    def bx_half(side, part):
        base = base_b(xm if side == 0 else xp, c, y2) + part * half_z
        wait(kv.at[pl.ds(base, half_z)], r_bxh.at[side, part])
        if side == part:
            push("b", base, half_z, r_bx2.at[side, 3], x_plus if side == 0 else x_minus)
        push("b", base, half_z, r_bs, sib)

    def bx_far(side, row):
        yy = y2 if row == 3 else b_rows[row]
        base = base_b(x2, c, yy) + side * half_z
        wait(kv.at[pl.ds(base, half_z)], r_bx2.at[side, row])
        push("b", base, half_z, r_bs, sib)

    b_own()
    a_own(0)
    b_from(0)
    b_from(1)
    a_own(1)
    a_own(7)
    b_far(0)
    b_far(1)
    for side in (0, 1):
        a_from(side, 0)
        bx_from(side, 0)
    a_own(2)
    a_own(6)
    for o in (1, 7):
        a_from(0, o)
        a_from(1, o)
    a_own(3)
    a_own(5)
    for side in (0, 1):
        bx_from(side, 1)
    a_own(4)
    for o in (2, 6):
        a_from(0, o)
        a_from(1, o)
    for side in (0, 1):
        bx_from(side, 2)
    for o in (3, 5, 4):
        a_from(0, o)
        a_from(1, o)
    for side in (0, 1):
        for part in (0, 1):
            bx_half(side, part)
    for o in ORDER:
        a_far(o)
    for row in range(4):
        bx_far(0, row)
        bx_far(1, row)

    wait(meta_v.at[0], l_m)
    wait(meta_v.at[pl.ds(0, NZ - 1)], r_m)
    to_smem = pltpu.make_async_copy(meta_v, meta_s, l_s)
    to_smem.start()
    to_smem.wait()
    units = NZ * NX + NZ
    wait(qv.at[pl.ds(0, 2)], l_q)
    wait(qv.at[pl.ds(0, units - 2)], r_q)
    wait(kv.at[pl.ds(0, NBLOCKS // 2)], r_as)
    wait(kv.at[pl.ds(0, NBLOCKS // 2)], r_bs)

    key_ids = lax.broadcasted_iota(jnp.int32, (BL, 2 * BL), 1)

    def place(t):
        is_b = t >= NZ * NX
        i = jnp.where(is_b, t - NZ * NX, div(t, NX))
        far = jnp.where(rem(i, 2) == 1, NZ - div(i + 1, 2), div(i, 2))
        zz = rem(z + NZ // 2 + far, NZ)
        xx = jnp.where(is_b, x, rem(x + rem(t, NX), NX))
        unit = jnp.where(is_b, NZ * NX + zz, zz * NX + xx)
        return is_b, zz, xx, unit

    def attend(t):
        is_b, zz, xx, unit = place(t)
        row = xx * NC + c
        lane = jnp.where(is_b, SLOT_B_LANE, 0)
        count = meta_s[zz, row, COUNT_LANE]
        slots = [meta_s[zz, row, lane + e] for e in range(LIST_LEN)]
        q = qv[unit]
        top = None
        for p in range(LIST_LEN // 2):
            keys = jnp.concatenate([kv[slots[2 * p], 0], kv[slots[2 * p + 1], 0]], axis=0)
            scores = lax.dot_general(q, keys, (((1,), (1,)), ((), ())), preferred_element_type=jnp.float32)
            if p >= 2:
                scores = jnp.where(key_ids < (count - 2 * p) * BL, scores, -jnp.inf)
            s_ref[p] = scores
            top = scores if top is None else jnp.maximum(top, scores)
        row_max = jnp.max(top, axis=1, keepdims=True)
        total = None
        blended = None
        for p in range(LIST_LEN // 2):
            weights = jnp.exp2((s_ref[p] - row_max) * EXP2_SCALE)
            vals = jnp.concatenate([kv[slots[2 * p], 1], kv[slots[2 * p + 1], 1]], axis=0)
            part = jnp.dot(weights.astype(jnp.bfloat16), vals, preferred_element_type=jnp.float32)
            blended = part if blended is None else blended + part
            total = weights if total is None else total + weights
        weight_sum = jnp.sum(total, axis=1, keepdims=True)
        ov[unit] = (blended / weight_sum).astype(jnp.bfloat16)

    def give(t):
        is_b, zz, xx, unit = place(t)
        dst = out_ref.at[:, cols(jnp.where(is_b, head_b, head_a))]
        mine = (zz == z) & (xx == x)

        @pl.when(mine)
        def _():
            local(ov.at[unit], dst, l_o)

        @pl.when(jnp.logical_not(mine))
        def _():
            remote(ov.at[unit], dst, s_o, r_o, dev(zz, y, xx, c))

    def work(t, carry):
        attend(t)

        @pl.when(t > 0)
        def _():
            give(t - 1)

        return carry

    lax.fori_loop(0, units, work, 0)
    give(jnp.int32(units - 1))

    wait(qv.at[pl.ds(0, units - 2)], r_o)
    wait(qv.at[pl.ds(0, 2)], l_o)
    wait(qv.at[pl.ds(0, units - 2)], s_o)
    wait(meta_v.at[pl.ds(0, NZ - 1)], s_m)
    wait(kv.at[pl.ds(0, (units - 2) * 3 // 2)], s_1)
    wait(kv.at[pl.ds(0, sent["a"])], s_a)
    wait(kv.at[pl.ds(0, sent["b"])], s_b)


def body(queries, keys, values, block_lists, block_counts):
    zz, rest = block_lists // (NY * NX * NC), block_lists % (NY * NX * NC)
    yy, rest = rest // (NX * NC), rest % (NX * NC)
    xx, cc = rest // NC, rest % NC
    slot_a = ((yy * NC + cc) * NZ + zz) * NX + xx
    slot_b = NBLOCKS + ((xx * NC + cc) * NY + yy) * NZ + zz
    rows = block_lists.shape[0]
    gap = jnp.zeros((rows, SLOT_B_LANE - LIST_LEN), jnp.int32)
    meta = jnp.concatenate(
        [slot_a, gap, slot_b, gap, block_counts[:, None], jnp.zeros((rows, 128 - COUNT_LANE - 1), jnp.int32)], axis=1
    )
    dma = pltpu.SemaphoreType.DMA
    units = NZ * NX + NZ
    return pl.pallas_call(
        kernel,
        out_shape=jax.ShapeDtypeStruct(queries.shape, jnp.bfloat16),
        in_specs=[pl.BlockSpec(memory_space=pl.ANY)] * 4,
        out_specs=pl.BlockSpec(memory_space=pl.ANY),
        scratch_shapes=[
            pltpu.VMEM((2 * NBLOCKS, 2, BL, HD), jnp.bfloat16),
            pltpu.VMEM((units, BL, HD), jnp.bfloat16),
            pltpu.VMEM((units, BL, HD), jnp.bfloat16),
            pltpu.VMEM((NZ, NX * NC, 128), jnp.int32),
            pltpu.SMEM((NZ, NX * NC, 128), jnp.int32),
            pltpu.VMEM((LIST_LEN // 2, BL, 2 * BL), jnp.float32),
            dma((2,)), dma, dma, dma, dma,
            dma, dma, dma, dma, dma,
            dma((NZ,)), dma, dma, dma, dma,
            dma((2, NZ)), dma((NZ,)), dma,
            dma((2,)), dma((2,)), dma, dma((2, 3)), dma((2, 2)), dma((2, 4)),
        ],
        compiler_params=pltpu.CompilerParams(collective_id=0, has_side_effects=True, vmem_limit_bytes=52 << 20),
    )(queries, keys, values, meta)


def solution(mesh):
    placed = (
        P(("seq", "uly"), None),
        P(("seq", "uly"), None),
        P(("seq", "uly"), None),
        P("seq", None),
        P("seq"),
    )
    return jax.shard_map(
        body, mesh=mesh, in_specs=placed, out_specs=P(("seq", "uly"), None), check_vma=False
    )
```

```python
import jax
import jax.numpy as jnp
from jax import lax
from jax.experimental import pallas as pl
from jax.experimental.pallas import tpu as pltpu
from jax.sharding import PartitionSpec as P

NZ, NY, NX, NC = 8, 4, 4, 2
HD = 128
BL = 128
LIST_LEN = 12
NBLOCKS = NZ * NY * NX * NC
PLANE_HEADS = NX + 1
MESH = pl.DeviceIdType.MESH
EXP2_SCALE = HD ** (-0.5) * 1.4426950408889634
ORDER = (0, 1, 7, 2, 6, 3, 5, 4)
NEAR = 2
LAST = (NZ - 1) * NX // 2
SLOT_B_LANE = 16
COUNT_LANE = 32


def rem(a, n):
    return lax.rem(a, jnp.int32(n))


def div(a, n):
    return lax.div(a, jnp.int32(n))


def kernel(q_ref, k_ref, v_ref, meta_ref, out_ref, kva, kvb, qv, ov, meta_v, meta_s, s_ref, l_kv, l_q, l_m, l_o, l_s,
           s_1, s_q, s_m, s_a, s_b, s_o, r_a1, r_b1, r_q, r_qb, r_m, r_o, r_ay, r_ay2, r_as, r_by, r_by2, r_bs, r_bx, r_bxh, r_bx2,
           r_cx, r_cx2, r_cy, r_cy2):
    s = lax.axis_index("seq")
    u = lax.axis_index("uly")
    z, y = div(s, NY), rem(s, NY)
    x, c = div(u, NC), rem(u, NC)

    def dev(z2, y2, x2, c2):
        return (z2 * NY + y2, x2 * NC + c2)

    yp, ym = rem(y + 1, NY), rem(y + NY - 1, NY)
    y2 = rem(y + 2, NY)
    xp, xm = rem(x + 1, NX), rem(x + NX - 1, NX)
    x2 = rem(x + 2, NX)
    sib = dev(z, y, x, 1 - c)
    y_plus, y_minus = dev(z, yp, x, c), dev(z, ym, x, c)
    x_plus, x_minus = dev(z, y, xp, c), dev(z, y, xm, c)

    def slot_a(zz, yy, xx, cc):
        return ((yy * NC + cc) * NZ + zz) * NX + xx

    def base_b(xx, cc, yy):
        return ((xx * NC + cc) * NY + yy) * NZ

    def place_of(o):
        return jnp.where(o <= NZ // 2, jnp.maximum(2 * o - 1, 0), 2 * (NZ - o))

    def cols(h):
        return pl.ds(pl.multiple_of(h * HD, HD), HD)

    def wait(ref, sem):
        pltpu.make_async_copy(ref, ref, sem).wait()

    def local(src, dst, sem):
        pltpu.make_async_copy(src, dst, sem).start()

    def remote(src, dst, send, recv, target):
        pltpu.make_async_remote_copy(
            src_ref=src, dst_ref=dst, send_sem=send, recv_sem=recv, device_id=target, device_id_type=MESH
        ).start()

    me_a = slot_a(z, y, x, c)
    me_b = base_b(x, c, y)
    head_a, head_b = PLANE_HEADS * z + x, PLANE_HEADS * z + NX
    local(meta_ref, meta_v.at[z], l_m)
    local(k_ref.at[:, cols(head_b)], kvb.at[me_b, 0], l_kv.at[1])
    local(v_ref.at[:, cols(head_b)], kvb.at[me_b, 1], l_kv.at[1])
    local(k_ref.at[:, cols(head_a)], kva.at[me_a, 0], l_kv.at[0])
    local(v_ref.at[:, cols(head_a)], kva.at[me_a, 1], l_kv.at[0])
    local(q_ref.at[:, cols(head_a)], qv.at[z * NX + x], l_q.at[0])
    local(q_ref.at[:, cols(head_b)], qv.at[NZ * NX + z], l_q.at[1])

    barrier = pltpu.get_barrier_semaphore()

    def greet(i, carry):
        zz, xx = rem(z + div(i, NX), NZ), rem(x + rem(i, NX), NX)
        pl.semaphore_signal(barrier, inc=1, device_id=dev(zz, y, xx, c), device_id_type=MESH)
        return carry

    lax.fori_loop(1, NZ * NX, greet, 0)
    for target in (sib, y_plus, y_minus):
        pl.semaphore_signal(barrier, inc=1, device_id=target, device_id_type=MESH)
    pl.semaphore_wait(barrier, NZ * NX - 1 + 3)

    sent = {"a": 0, "b": 0}

    def push(which, start, n, recv, target):
        part = (kva if which == "a" else kvb).at[pl.ds(start, n)]
        sent[which] += n
        remote(part, part, s_a if which == "a" else s_b, recv, target)

    def a_one(at):
        push("a", at, 1, r_ay.at[0, 0], y_plus)
        push("a", at, 1, r_ay.at[1, 0], y_minus)
        push("a", at, 1, r_as, sib)

    def a_own(o):
        base = slot_a(rem(z + o, NZ), y, 0, c)
        if o == 0:
            wait(kva.at[pl.ds(base, NX - 1)], r_a1.at[0])
            for r in range(1, NX):
                a_one(slot_a(z, y, rem(x + r, NX), c))
            return
        wait(kva.at[pl.ds(base, NX)], r_a1.at[o])
        push("a", base, NX, r_ay.at[0, o], y_plus)
        push("a", base, NX, r_ay.at[1, o], y_minus)
        push("a", base, NX, r_as, sib)

    def a_from(side, o):
        base = slot_a(rem(z + o, NZ), ym if side == 0 else yp, 0, c)
        wait(kva.at[pl.ds(base, NX)], r_ay.at[side, o])
        if (o < NZ // 2) == (side == 0):
            push("a", base, NX, r_ay2.at[o], y_plus if side == 0 else y_minus)
        push("a", base, NX, r_as, sib)

    def a_far(o):
        base = slot_a(rem(z + o, NZ), y2, 0, c)
        wait(kva.at[pl.ds(base, NX)], r_ay2.at[o])
        push("a", base, NX, r_as, sib)

    near, rest = NEAR, NZ - NEAR
    half_n, half_r = near // 2, rest // 2
    b_rows = (y, ym, yp, y2)
    b_cols = (x, xm, xp, x2)

    def b_row(p):
        push("b", base_b(x, c, y) + p, 1, r_cy.at[0, 0], y_plus)
        push("b", base_b(x, c, y) + p, 1, r_cy.at[1, 0], y_minus)

    def b_own(p):
        base = base_b(x, c, y)
        if p == 0:
            wait(kvb.at[base], l_kv.at[1])
        else:
            wait(kvb.at[base + p], r_b1.at[p])
        if p < near:
            push("b", base + p, 1, r_cx.at[0], x_plus)
            push("b", base + p, 1, r_cx.at[1], x_minus)
            if p == 0:
                b_row(p)
        else:
            push("b", base + p, 1, r_by.at[0], y_plus)
            push("b", base + p, 1, r_by.at[1], y_minus)
            push("b", base + p, 1, r_bx.at[0, 0], x_plus)
            push("b", base + p, 1, r_bx.at[1, 0], x_minus)
        push("b", base + p, 1, r_bs, sib)

    def b_from(side):
        base = base_b(x, c, b_rows[1 + side]) + near
        wait(kvb.at[pl.ds(base, rest)], r_by.at[side])
        push("b", base + side * half_r, half_r, r_by2.at[side], y_minus if side else y_plus)
        push("b", base, rest, r_bx.at[0, 1 + side], x_plus)
        push("b", base, rest, r_bx.at[1, 1 + side], x_minus)
        push("b", base, rest, r_bs, sib)

    def b_far(part):
        base = base_b(x, c, y2) + near + part * half_r
        wait(kvb.at[pl.ds(base, half_r)], r_by2.at[part])
        push("b", base, half_r, r_bxh.at[0, part], x_plus)
        push("b", base, half_r, r_bxh.at[1, part], x_minus)
        push("b", base, half_r, r_bs, sib)

    def bx_from(side, row):
        base = base_b(b_cols[1 + side], c, b_rows[row]) + near
        wait(kvb.at[pl.ds(base, rest)], r_bx.at[side, row])
        push("b", base + side * half_r, half_r, r_bx2.at[side, row], x_minus if side else x_plus)
        push("b", base, rest, r_bs, sib)

    def bx_half(side, part):
        base = base_b(b_cols[1 + side], c, y2) + near + part * half_r
        wait(kvb.at[pl.ds(base, half_r)], r_bxh.at[side, part])
        if side == part:
            push("b", base, half_r, r_bx2.at[side, 3], x_minus if side else x_plus)
        push("b", base, half_r, r_bs, sib)

    def bx_far(side, row):
        base = base_b(x2, c, b_rows[row]) + near + side * half_r
        wait(kvb.at[pl.ds(base, half_r)], r_bx2.at[side, row])
        push("b", base, half_r, r_bs, sib)

    def c_from(side):
        base = base_b(b_cols[1 + side], c, y)
        wait(kvb.at[pl.ds(base, near)], r_cx.at[side])
        push("b", base + side * half_n, half_n, r_cx2.at[side], x_minus if side else x_plus)
        push("b", base, near, r_bs, sib)

    def c_far(part):
        base = base_b(x2, c, y) + part * half_n
        wait(kvb.at[pl.ds(base, half_n)], r_cx2.at[part])
        push("b", base, half_n, r_bs, sib)

    def c_spread(col):
        base = base_b(b_cols[col], c, y)
        push("b", base, near, r_cy.at[0, col], y_plus)
        push("b", base, near, r_cy.at[1, col], y_minus)

    def cy_from(side, col):
        base = base_b(b_cols[col], c, b_rows[1 + side])
        wait(kvb.at[pl.ds(base, near)], r_cy.at[side, col])
        push("b", base + side * half_n, half_n, r_cy2.at[side, col], y_minus if side else y_plus)
        push("b", base, near, r_bs, sib)

    def cy_far(side, col):
        base = base_b(b_cols[col], c, y2) + side * half_n
        wait(kvb.at[pl.ds(base, half_n)], r_cy2.at[side, col])
        push("b", base, half_n, r_bs, sib)

    wait(kva.at[me_a], l_kv.at[0])
    a_one(me_a)
    b_own(0)

    def step_to(j):
        half = div(j + 1, 2)
        return jnp.where(rem(j, 2) == 1, half, NZ - half)

    def send_meta_b(j, carry):
        t = step_to(j)
        zz = rem(z + t, NZ)
        target = dev(zz, y, x, c)
        h = PLANE_HEADS * zz + NX
        remote(meta_ref, meta_v.at[z], s_m, r_m, target)
        there = me_b + place_of(NZ - t)
        remote(k_ref.at[:, cols(h)], kvb.at[there, 0], s_1, r_b1.at[place_of(NZ - t)], target)
        remote(v_ref.at[:, cols(h)], kvb.at[there, 1], s_1, r_b1.at[place_of(NZ - t)], target)
        return carry

    lax.fori_loop(1, NZ, send_meta_b, 0)

    def send_a(i, carry):
        j = div(i, NX)
        t = jnp.where(j == 0, 0, step_to(j))
        zz, xx = rem(z + t, NZ), rem(x + rem(i, NX), NX)
        target = dev(zz, y, xx, c)
        h = PLANE_HEADS * zz + xx
        o = rem(NZ - t, NZ)
        remote(k_ref.at[:, cols(h)], kva.at[me_a, 0], s_1, r_a1.at[o], target)
        remote(v_ref.at[:, cols(h)], kva.at[me_a, 1], s_1, r_a1.at[o], target)
        return carry

    lax.fori_loop(1, NZ * NX, send_a, 0)

    def send_q(i, carry):
        j = div(i, NX)
        t = jnp.where(j == 0, 0, step_to(j))
        zz, xx = rem(z + t, NZ), rem(x + rem(i, NX), NX)
        remote(q_ref.at[:, cols(PLANE_HEADS * zz + xx)], qv.at[z * NX + x], s_q, r_q.at[rem(NZ - t, NZ)], dev(zz, y, xx, c))
        return carry

    lax.fori_loop(1, NZ * NX, send_q, 0)

    def send_qb(j, carry):
        zz = rem(z + step_to(j), NZ)
        remote(q_ref.at[:, cols(PLANE_HEADS * zz + NX)], qv.at[NZ * NX + z], s_q, r_qb, dev(zz, y, x, c))
        return carry

    lax.fori_loop(1, NZ, send_qb, 0)

    def both(f, *args):
        for side in (0, 1):
            f(side, *args)

    b_own(1)
    a_own(0)
    for p in range(2, NZ):
        b_own(p)
    a_own(1)
    a_own(7)
    both(b_from)
    both(c_from)
    both(a_from, 0)
    a_own(2)
    both(bx_from, 0)
    a_own(6)
    both(a_from, 1)
    both(b_far)
    both(a_from, 7)
    a_own(3)
    both(bx_from, 1)
    a_own(5)
    both(a_from, 2)
    both(a_from, 6)
    a_own(4)
    for o in (0, 1, 7):
        a_far(o)
    both(a_from, 3)
    both(c_far)
    both(bx_from, 2)
    both(a_from, 5)
    for o in (2, 6):
        a_far(o)
    both(a_from, 4)
    b_row(1)
    for col in (1, 2, 3):
        c_spread(col)
    both(bx_half, 0)
    both(bx_half, 1)
    for o in (3, 5, 4):
        a_far(o)

    wait(meta_v.at[0], l_m)
    wait(meta_v.at[pl.ds(0, NZ - 1)], r_m)
    to_smem = pltpu.make_async_copy(meta_v, meta_s, l_s)
    to_smem.start()
    to_smem.wait()
    wait(kva.at[pl.ds(0, NBLOCKS // 2)], r_as)

    key_ids = lax.broadcasted_iota(jnp.int32, (BL, 2 * BL), 1)

    def weigh(kv, part, row, lane, zz, unit):
        count = meta_s[zz, row, COUNT_LANE]
        slots = [meta_s[zz, row, lane + e] for e in range(LIST_LEN)]
        if lane:
            slots = [n // NZ * NZ + place_of(rem(n % NZ + NZ - z, NZ)) for n in slots]
        q = qv[unit]
        top = None
        for p in range(LIST_LEN // 2):
            keys = jnp.concatenate([kv[slots[2 * p], 0], kv[slots[2 * p + 1], 0]], axis=0)
            scores = lax.dot_general(q, keys, (((1,), (1,)), ((), ())), preferred_element_type=jnp.float32)
            if p >= 2:
                scores = jnp.where(key_ids < (count - 2 * p) * BL, scores, -jnp.inf)
            s_ref[part, p] = scores
            top = scores if top is None else jnp.maximum(top, scores)
        return slots, jnp.max(top, axis=1, keepdims=True)

    def blend(kv, part, unit, slots, row_max):
        total = None
        blended = None
        for p in range(LIST_LEN // 2):
            weights = jnp.exp2((s_ref[part, p] - row_max) * EXP2_SCALE)
            vals = jnp.concatenate([kv[slots[2 * p], 1], kv[slots[2 * p + 1], 1]], axis=0)
            piece = jnp.dot(weights.astype(jnp.bfloat16), vals, preferred_element_type=jnp.float32)
            blended = piece if blended is None else blended + piece
            total = weights if total is None else total + weights
        weight_sum = jnp.sum(total, axis=1, keepdims=True)
        ov[unit] = (blended / weight_sum).astype(jnp.bfloat16)

    def attend(kv, lane, picks):
        state = [weigh(kv, n, row, lane, zz, unit) for n, (row, zz, unit) in enumerate(picks)]
        for n, (row, zz, unit) in enumerate(picks):
            blend(kv, n, unit, *state[n])

    def give(zz, xx, unit, head):
        dst = out_ref.at[:, cols(head)]
        mine = (zz == z) & (xx == x)

        @pl.when(mine)
        def _():
            local(ov.at[unit], dst, l_o)

        @pl.when(jnp.logical_not(mine))
        def _():
            remote(ov.at[unit], dst, s_o, r_o, dev(zz, y, xx, c))

    def turn(g):
        return jnp.where(rem(g, 2) == 1, NZ // 2 - div(g + 1, 2), NZ // 2 + div(g, 2))

    def give_a(t):
        zz = rem(z + turn(div(t, NX)), NZ)
        xx = rem(x + rem(t, NX), NX)
        give(zz, xx, zz * NX + xx, head_a)

    def give_b(t):
        zz = rem(z + turn(t), NZ)
        give(zz, x, NZ * NX + zz, head_b)

    def work_a(i, carry):
        picks = []
        for t in (2 * i, 2 * i + 1):
            zz = rem(z + turn(div(t, NX)), NZ)
            xx = rem(x + rem(t, NX), NX)
            picks.append((xx * NC + c, zz, zz * NX + xx))
        attend(kva, 0, picks)

        @pl.when((i > 0) & (i != LAST))
        def _():
            give_a(2 * i - 2)
            give_a(2 * i - 1)

        return carry

    def work_b(i, carry):
        picks = []
        for t in (2 * i, 2 * i + 1):
            zz = rem(z + turn(t), NZ)
            picks.append((x * NC + c, zz, NZ * NX + zz))
        attend(kvb, SLOT_B_LANE, picks)

        @pl.when(i > 0)
        def _():
            give_b(2 * i - 2)
            give_b(2 * i - 1)

        return carry

    between = {
        0: [lambda: both(bx_far, 0), lambda: both(bx_far, 1)],
        1: [lambda: both(cy_from, 0), lambda: both(bx_far, 2)],
        2: [lambda: both(cy_from, 1), lambda: both(bx_far, 3)],
        3: [lambda: both(cy_from, 2)],
        4: [lambda: both(cy_from, 3)],
        5: [lambda: both(cy_far, 0), lambda: both(cy_far, 1)],
        6: [lambda: both(cy_far, 2), lambda: both(cy_far, 3)],
    }
    def group(g):
        o = (4, 3, 5, 2, 6, 1, 7, 0)[g]
        zz = rem(z + o, NZ)
        if o == 0:
            wait(qv.at[pl.ds(0, NX - 1)], r_q.at[0])
            wait(qv.at[0], l_q.at[0])
        else:
            wait(qv.at[pl.ds(zz * NX, NX)], r_q.at[o])
        lax.fori_loop(g * NX // 2, (g + 1) * NX // 2, work_a, 0)

    for g in range(NZ - 1):
        group(g)
        for event in between.get(g, []):
            event()
    give_a(jnp.int32(2 * LAST - 2))
    give_a(jnp.int32(2 * LAST - 1))

    wait(qv.at[NZ * NX], l_q.at[1])
    wait(qv.at[pl.ds(NZ * NX, NZ - 1)], r_qb)
    wait(kvb.at[pl.ds(0, NBLOCKS // 2)], r_bs)
    lax.fori_loop(0, NZ // 2, work_b, 0)
    give_b(jnp.int32(NZ - 2))
    give_b(jnp.int32(NZ - 1))
    group(NZ - 1)
    give_a(jnp.int32(NZ * NX - 2))
    give_a(jnp.int32(NZ * NX - 1))

    units = NZ * NX + NZ
    wait(qv.at[pl.ds(0, units - 2)], r_o)
    wait(qv.at[pl.ds(0, 2)], l_o)
    wait(qv.at[pl.ds(0, units - 2)], s_o)
    wait(qv.at[pl.ds(0, units - 2)], s_q)
    wait(meta_v.at[pl.ds(0, NZ - 1)], s_m)
    wait(kva.at[pl.ds(0, units - 2)], s_1)
    wait(kva.at[pl.ds(0, sent["a"])], s_a)
    wait(kvb.at[pl.ds(0, sent["b"])], s_b)


def body(queries, keys, values, block_lists, block_counts):
    zz, rest = block_lists // (NY * NX * NC), block_lists % (NY * NX * NC)
    yy, rest = rest // (NX * NC), rest % (NX * NC)
    xx, cc = rest // NC, rest % NC
    slot_a = ((yy * NC + cc) * NZ + zz) * NX + xx
    slot_b = ((xx * NC + cc) * NY + yy) * NZ + zz
    rows = block_lists.shape[0]
    gap = jnp.zeros((rows, SLOT_B_LANE - LIST_LEN), jnp.int32)
    meta = jnp.concatenate(
        [slot_a, gap, slot_b, gap, block_counts[:, None], jnp.zeros((rows, 128 - COUNT_LANE - 1), jnp.int32)], axis=1
    )
    dma = pltpu.SemaphoreType.DMA
    units = NZ * NX + NZ
    return pl.pallas_call(
        kernel,
        out_shape=jax.ShapeDtypeStruct(queries.shape, jnp.bfloat16),
        in_specs=[pl.BlockSpec(memory_space=pl.ANY)] * 4,
        out_specs=pl.BlockSpec(memory_space=pl.ANY),
        scratch_shapes=[
            pltpu.VMEM((NBLOCKS, 2, BL, HD), jnp.bfloat16),
            pltpu.VMEM((NBLOCKS, 2, BL, HD), jnp.bfloat16),
            pltpu.VMEM((units, BL, HD), jnp.bfloat16),
            pltpu.VMEM((units, BL, HD), jnp.bfloat16),
            pltpu.VMEM((NZ, NX * NC, 128), jnp.int32),
            pltpu.SMEM((NZ, NX * NC, 128), jnp.int32),
            pltpu.VMEM((2, LIST_LEN // 2, BL, 2 * BL), jnp.float32),
            dma((2,)), dma((2,)), dma, dma, dma,
            dma, dma, dma, dma, dma, dma,
            dma((NZ,)), dma((NZ,)), dma((NZ,)), dma, dma, dma,
            dma((2, NZ)), dma((NZ,)), dma,
            dma((2,)), dma((2,)), dma, dma((2, 3)), dma((2, 2)), dma((2, 4)),
            dma((2,)), dma((2,)), dma((2, 4)), dma((2, 4)),
        ],
        compiler_params=pltpu.CompilerParams(collective_id=0, has_side_effects=True, vmem_limit_bytes=52 << 20),
    )(queries, keys, values, meta)


def solution(mesh):
    placed = (
        P(("seq", "uly"), None),
        P(("seq", "uly"), None),
        P(("seq", "uly"), None),
        P("seq", None),
        P("seq"),
    )
    return jax.shard_map(
        body, mesh=mesh, in_specs=placed, out_specs=P(("seq", "uly"), None), check_vma=False
    )
```

```python
import jax
import jax.numpy as jnp
from jax import lax
from jax.experimental import pallas as pl
from jax.experimental.pallas import tpu as pltpu
from jax.sharding import PartitionSpec as P

NZ, NY, NX, NC = 8, 4, 4, 2
HD = 128
BL = 128
LIST_LEN = 12
NBLOCKS = NZ * NY * NX * NC
PLANE_HEADS = NX + 1
MESH = pl.DeviceIdType.MESH
EXP2_SCALE = HD ** (-0.5) * 1.4426950408889634
ORDER = (0, 1, 7, 2, 6, 3, 5, 4)
NEAR = 2
LAST = (NZ - 1) * NX // 2
SLOT_B_LANE = 16
COUNT_ROW = NX * NC


def rem(a, n):
    return lax.rem(a, jnp.int32(n))


def div(a, n):
    return lax.div(a, jnp.int32(n))


def kernel(q_ref, k_ref, v_ref, meta_ref, out_ref, kva, kvb, qv, ov, meta_v, meta_s, s_ref, l_kv, l_q, l_m, l_o, l_s,
           s_1, s_q, s_m, s_a, s_b, s_o, r_a1, r_b1, r_q, r_qb, r_m, r_o, r_ay, r_ay2, r_as, r_by, r_by2, r_bs, r_bx, r_bxh, r_bx2,
           r_cx, r_cx2, r_cy, r_cy2):
    s = lax.axis_index("seq")
    u = lax.axis_index("uly")
    z, y = div(s, NY), rem(s, NY)
    x, c = div(u, NC), rem(u, NC)

    def dev(z2, y2, x2, c2):
        return (z2 * NY + y2, x2 * NC + c2)

    yp, ym = rem(y + 1, NY), rem(y + NY - 1, NY)
    y2 = rem(y + 2, NY)
    xp, xm = rem(x + 1, NX), rem(x + NX - 1, NX)
    x2 = rem(x + 2, NX)
    sib = dev(z, y, x, 1 - c)
    y_plus, y_minus = dev(z, yp, x, c), dev(z, ym, x, c)
    x_plus, x_minus = dev(z, y, xp, c), dev(z, y, xm, c)

    def slot_a(zz, yy, xx, cc):
        return ((yy * NC + cc) * NZ + zz) * NX + xx

    def base_b(xx, cc, yy):
        return ((xx * NC + cc) * NY + yy) * NZ

    def place_of(o):
        return jnp.where(o <= NZ // 2, jnp.maximum(2 * o - 1, 0), 2 * (NZ - o))

    def cols(h):
        return pl.ds(pl.multiple_of(h * HD, HD), HD)

    def wait(ref, sem):
        pltpu.make_async_copy(ref, ref, sem).wait()

    def local(src, dst, sem):
        pltpu.make_async_copy(src, dst, sem).start()

    def remote(src, dst, send, recv, target):
        pltpu.make_async_remote_copy(
            src_ref=src, dst_ref=dst, send_sem=send, recv_sem=recv, device_id=target, device_id_type=MESH
        ).start()

    me_a = slot_a(z, y, x, c)
    me_b = base_b(x, c, y)
    head_a, head_b = PLANE_HEADS * z + x, PLANE_HEADS * z + NX
    local(meta_ref, meta_v.at[z], l_m)
    local(k_ref.at[:, cols(head_b)], kvb.at[me_b, 0], l_kv.at[1])
    local(v_ref.at[:, cols(head_b)], kvb.at[me_b, 1], l_kv.at[1])
    local(k_ref.at[:, cols(head_a)], kva.at[me_a, 0], l_kv.at[0])
    local(v_ref.at[:, cols(head_a)], kva.at[me_a, 1], l_kv.at[0])
    local(q_ref.at[:, cols(head_a)], qv.at[z * NX + x], l_q.at[0])
    local(q_ref.at[:, cols(head_b)], qv.at[NZ * NX + z], l_q.at[1])

    barrier = pltpu.get_barrier_semaphore()

    def greet(i, carry):
        zz, xx = rem(z + div(i, NX), NZ), rem(x + rem(i, NX), NX)
        pl.semaphore_signal(barrier, inc=1, device_id=dev(zz, y, xx, c), device_id_type=MESH)
        return carry

    lax.fori_loop(1, NZ * NX, greet, 0)
    for target in (sib, y_plus, y_minus):
        pl.semaphore_signal(barrier, inc=1, device_id=target, device_id_type=MESH)
    pl.semaphore_wait(barrier, NZ * NX - 1 + 3)

    sent = {"a": 0, "b": 0}

    def push(which, start, n, recv, target):
        part = (kva if which == "a" else kvb).at[pl.ds(start, n)]
        sent[which] += n
        remote(part, part, s_a if which == "a" else s_b, recv, target)

    def a_one(at):
        push("a", at, 1, r_ay.at[0, 0], y_plus)
        push("a", at, 1, r_ay.at[1, 0], y_minus)
        push("a", at, 1, r_as, sib)

    def a_own(o):
        base = slot_a(rem(z + o, NZ), y, 0, c)
        if o == 0:
            wait(kva.at[pl.ds(base, NX - 1)], r_a1.at[0])
            for r in range(1, NX):
                a_one(slot_a(z, y, rem(x + r, NX), c))
            return
        wait(kva.at[pl.ds(base, NX)], r_a1.at[o])
        push("a", base, NX, r_ay.at[0, o], y_plus)
        push("a", base, NX, r_ay.at[1, o], y_minus)
        push("a", base, NX, r_as, sib)

    def a_from(side, o):
        base = slot_a(rem(z + o, NZ), ym if side == 0 else yp, 0, c)
        wait(kva.at[pl.ds(base, NX)], r_ay.at[side, o])
        if (o < NZ // 2) == (side == 0):
            push("a", base, NX, r_ay2.at[o], y_plus if side == 0 else y_minus)
        push("a", base, NX, r_as, sib)

    def a_far(o):
        base = slot_a(rem(z + o, NZ), y2, 0, c)
        wait(kva.at[pl.ds(base, NX)], r_ay2.at[o])
        push("a", base, NX, r_as, sib)

    near, rest = NEAR, NZ - NEAR
    half_n, half_r = near // 2, rest // 2
    b_rows = (y, ym, yp, y2)
    b_cols = (x, xm, xp, x2)

    def b_row(p):
        push("b", base_b(x, c, y) + p, 1, r_cy.at[0, 0], y_plus)
        push("b", base_b(x, c, y) + p, 1, r_cy.at[1, 0], y_minus)

    def b_own(p):
        base = base_b(x, c, y)
        if p == 0:
            wait(kvb.at[base], l_kv.at[1])
        else:
            wait(kvb.at[base + p], r_b1.at[p])
        if p < near:
            push("b", base + p, 1, r_cx.at[0], x_plus)
            push("b", base + p, 1, r_cx.at[1], x_minus)
            if p == 0:
                b_row(p)
        else:
            push("b", base + p, 1, r_by.at[0], y_plus)
            push("b", base + p, 1, r_by.at[1], y_minus)
            push("b", base + p, 1, r_bx.at[0, 0], x_plus)
            push("b", base + p, 1, r_bx.at[1, 0], x_minus)
        push("b", base + p, 1, r_bs, sib)

    def b_from(side):
        base = base_b(x, c, b_rows[1 + side]) + near
        wait(kvb.at[pl.ds(base, rest)], r_by.at[side])
        push("b", base + side * half_r, half_r, r_by2.at[side], y_minus if side else y_plus)
        push("b", base, rest, r_bx.at[0, 1 + side], x_plus)
        push("b", base, rest, r_bx.at[1, 1 + side], x_minus)
        push("b", base, rest, r_bs, sib)

    def b_far(part):
        base = base_b(x, c, y2) + near + part * half_r
        wait(kvb.at[pl.ds(base, half_r)], r_by2.at[part])
        push("b", base, half_r, r_bxh.at[0, part], x_plus)
        push("b", base, half_r, r_bxh.at[1, part], x_minus)
        push("b", base, half_r, r_bs, sib)

    def bx_from(side, row):
        base = base_b(b_cols[1 + side], c, b_rows[row]) + near
        wait(kvb.at[pl.ds(base, rest)], r_bx.at[side, row])
        push("b", base + side * half_r, half_r, r_bx2.at[side, row], x_minus if side else x_plus)
        push("b", base, rest, r_bs, sib)

    def bx_half(side, part):
        base = base_b(b_cols[1 + side], c, y2) + near + part * half_r
        wait(kvb.at[pl.ds(base, half_r)], r_bxh.at[side, part])
        if side == part:
            push("b", base, half_r, r_bx2.at[side, 3], x_minus if side else x_plus)
        push("b", base, half_r, r_bs, sib)

    def bx_far(side, row):
        base = base_b(x2, c, b_rows[row]) + near + side * half_r
        wait(kvb.at[pl.ds(base, half_r)], r_bx2.at[side, row])
        push("b", base, half_r, r_bs, sib)

    def c_from(side):
        base = base_b(b_cols[1 + side], c, y)
        wait(kvb.at[pl.ds(base, near)], r_cx.at[side])
        push("b", base + side * half_n, half_n, r_cx2.at[side], x_minus if side else x_plus)
        push("b", base, near, r_bs, sib)

    def c_far(part):
        base = base_b(x2, c, y) + part * half_n
        wait(kvb.at[pl.ds(base, half_n)], r_cx2.at[part])
        push("b", base, half_n, r_bs, sib)

    def c_spread(col):
        base = base_b(b_cols[col], c, y)
        push("b", base, near, r_cy.at[0, col], y_plus)
        push("b", base, near, r_cy.at[1, col], y_minus)

    def cy_from(side, col):
        base = base_b(b_cols[col], c, b_rows[1 + side])
        wait(kvb.at[pl.ds(base, near)], r_cy.at[side, col])
        push("b", base + side * half_n, half_n, r_cy2.at[side, col], y_minus if side else y_plus)
        push("b", base, near, r_bs, sib)

    def cy_far(side, col):
        base = base_b(b_cols[col], c, y2) + side * half_n
        wait(kvb.at[pl.ds(base, half_n)], r_cy2.at[side, col])
        push("b", base, half_n, r_bs, sib)

    wait(kva.at[me_a], l_kv.at[0])
    a_one(me_a)
    b_own(0)

    def step_to(j):
        half = div(j + 1, 2)
        return jnp.where(rem(j, 2) == 1, half, NZ - half)

    def send_meta_b(j, carry):
        t = step_to(j)
        zz = rem(z + t, NZ)
        target = dev(zz, y, x, c)
        h = PLANE_HEADS * zz + NX
        remote(meta_ref, meta_v.at[z], s_m, r_m, target)
        there = me_b + place_of(NZ - t)
        remote(k_ref.at[:, cols(h)], kvb.at[there, 0], s_1, r_b1.at[place_of(NZ - t)], target)
        remote(v_ref.at[:, cols(h)], kvb.at[there, 1], s_1, r_b1.at[place_of(NZ - t)], target)
        return carry

    def send_a(i, carry):
        j = div(i, NX)
        t = jnp.where(j == 0, 0, step_to(j))
        zz, xx = rem(z + t, NZ), rem(x + rem(i, NX), NX)
        target = dev(zz, y, xx, c)
        h = PLANE_HEADS * zz + xx
        o = rem(NZ - t, NZ)
        remote(k_ref.at[:, cols(h)], kva.at[me_a, 0], s_1, r_a1.at[o], target)
        remote(v_ref.at[:, cols(h)], kva.at[me_a, 1], s_1, r_a1.at[o], target)
        return carry

    lax.fori_loop(1, NX, send_a, 0)
    lax.fori_loop(1, NZ, send_meta_b, 0)
    lax.fori_loop(NX, NZ * NX, send_a, 0)

    def send_q(i, carry):
        j = div(i, NX)
        t = jnp.where(j == 0, 0, step_to(j))
        zz, xx = rem(z + t, NZ), rem(x + rem(i, NX), NX)
        remote(q_ref.at[:, cols(PLANE_HEADS * zz + xx)], qv.at[z * NX + x], s_q, r_q.at[rem(NZ - t, NZ)], dev(zz, y, xx, c))
        return carry

    lax.fori_loop(1, NZ * NX, send_q, 0)

    def send_qb(j, carry):
        zz = rem(z + step_to(j), NZ)
        remote(q_ref.at[:, cols(PLANE_HEADS * zz + NX)], qv.at[NZ * NX + z], s_q, r_qb, dev(zz, y, x, c))
        return carry

    lax.fori_loop(1, NZ, send_qb, 0)

    def both(f, *args):
        for side in (0, 1):
            f(side, *args)

    b_own(1)
    a_own(0)
    for p in range(2, NZ):
        b_own(p)
    a_own(1)
    a_own(7)
    both(b_from)
    both(c_from)
    both(a_from, 0)
    a_own(2)
    both(bx_from, 0)
    a_own(6)
    both(a_from, 1)
    both(b_far)
    both(a_from, 7)
    a_own(3)
    both(bx_from, 1)
    a_own(5)
    both(a_from, 2)
    both(a_from, 6)
    a_own(4)
    for o in (0, 1, 7):
        a_far(o)
    both(a_from, 3)
    both(c_far)
    both(bx_from, 2)
    both(a_from, 5)
    for o in (2, 6):
        a_far(o)
    both(a_from, 4)
    b_row(1)
    for col in (1, 2, 3):
        c_spread(col)
    both(bx_half, 0)
    both(bx_half, 1)
    for o in (3, 5, 4):
        a_far(o)

    wait(meta_v.at[0], l_m)
    wait(meta_v.at[pl.ds(0, NZ - 1)], r_m)
    to_smem = pltpu.make_async_copy(meta_v, meta_s, l_s)
    to_smem.start()
    to_smem.wait()
    wait(kva.at[pl.ds(0, NBLOCKS // 2)], r_as)

    key_ids = lax.broadcasted_iota(jnp.int32, (BL, 2 * BL), 1)

    def weigh(kv, part, row, lane, zz, unit):
        count = meta_s[zz, COUNT_ROW, row]
        slots = [meta_s[zz, row, lane + e] for e in range(LIST_LEN)]
        if lane:
            slots = [n // NZ * NZ + place_of(rem(n % NZ + NZ - z, NZ)) for n in slots]
        q = qv[unit]
        top = None
        for p in range(LIST_LEN // 2):
            keys = jnp.concatenate([kv[slots[2 * p], 0], kv[slots[2 * p + 1], 0]], axis=0)
            scores = lax.dot_general(q, keys, (((1,), (1,)), ((), ())), preferred_element_type=jnp.float32)
            if p >= 2:
                scores = jnp.where(key_ids < (count - 2 * p) * BL, scores, -jnp.inf)
            s_ref[part, p] = scores
            top = scores if top is None else jnp.maximum(top, scores)
        return slots, jnp.max(top, axis=1, keepdims=True)

    def blend(kv, part, unit, slots, row_max):
        total = None
        blended = None
        for p in range(LIST_LEN // 2):
            weights = jnp.exp2((s_ref[part, p] - row_max) * EXP2_SCALE)
            vals = jnp.concatenate([kv[slots[2 * p], 1], kv[slots[2 * p + 1], 1]], axis=0)
            piece = jnp.dot(weights.astype(jnp.bfloat16), vals, preferred_element_type=jnp.float32)
            blended = piece if blended is None else blended + piece
            total = weights if total is None else total + weights
        weight_sum = jnp.sum(total, axis=1, keepdims=True)
        ov[unit] = (blended / weight_sum).astype(jnp.bfloat16)

    def attend(kv, lane, picks):
        state = [weigh(kv, n, row, lane, zz, unit) for n, (row, zz, unit) in enumerate(picks)]
        for n, (row, zz, unit) in enumerate(picks):
            blend(kv, n, unit, *state[n])

    def give(zz, xx, unit, head):
        dst = out_ref.at[:, cols(head)]
        mine = (zz == z) & (xx == x)

        @pl.when(mine)
        def _():
            local(ov.at[unit], dst, l_o)

        @pl.when(jnp.logical_not(mine))
        def _():
            remote(ov.at[unit], dst, s_o, r_o, dev(zz, y, xx, c))

    def turn(g):
        return jnp.where(rem(g, 2) == 1, NZ // 2 - div(g + 1, 2), NZ // 2 + div(g, 2))

    def give_a(t):
        zz = rem(z + turn(div(t, NX)), NZ)
        xx = rem(x + rem(t, NX), NX)
        give(zz, xx, zz * NX + xx, head_a)

    def give_b(t):
        zz = rem(z + turn(t), NZ)
        give(zz, x, NZ * NX + zz, head_b)

    def work_a(i, carry):
        picks = []
        for t in (2 * i, 2 * i + 1):
            zz = rem(z + turn(div(t, NX)), NZ)
            xx = rem(x + rem(t, NX), NX)
            picks.append((xx * NC + c, zz, zz * NX + xx))
        attend(kva, 0, picks)

        @pl.when((i > 0) & (i != LAST))
        def _():
            give_a(2 * i - 2)
            give_a(2 * i - 1)

        return carry

    def work_b(i, carry):
        picks = []
        for t in (2 * i, 2 * i + 1):
            zz = rem(z + turn(t), NZ)
            picks.append((x * NC + c, zz, NZ * NX + zz))
        attend(kvb, SLOT_B_LANE, picks)

        @pl.when(i > 0)
        def _():
            give_b(2 * i - 2)
            give_b(2 * i - 1)

        return carry

    between = {
        0: [lambda: both(bx_far, 0), lambda: both(bx_far, 1)],
        1: [lambda: both(cy_from, 0), lambda: both(bx_far, 2)],
        2: [lambda: both(cy_from, 1), lambda: both(bx_far, 3)],
        3: [lambda: both(cy_from, 2)],
        4: [lambda: both(cy_from, 3)],
        5: [lambda: both(cy_far, 0), lambda: both(cy_far, 1)],
        6: [lambda: both(cy_far, 2), lambda: both(cy_far, 3)],
    }
    def group(g):
        o = (4, 3, 5, 2, 6, 1, 7, 0)[g]
        zz = rem(z + o, NZ)
        if o == 0:
            wait(qv.at[pl.ds(0, NX - 1)], r_q.at[0])
            wait(qv.at[0], l_q.at[0])
        else:
            wait(qv.at[pl.ds(zz * NX, NX)], r_q.at[o])
        lax.fori_loop(g * NX // 2, (g + 1) * NX // 2, work_a, 0)

    for g in range(NZ - 1):
        group(g)
        for event in between.get(g, []):
            event()
    give_a(jnp.int32(2 * LAST - 2))
    give_a(jnp.int32(2 * LAST - 1))

    wait(qv.at[NZ * NX], l_q.at[1])
    wait(qv.at[pl.ds(NZ * NX, NZ - 1)], r_qb)
    wait(kvb.at[pl.ds(0, NBLOCKS // 2)], r_bs)
    lax.fori_loop(0, NZ // 2, work_b, 0)
    give_b(jnp.int32(NZ - 2))
    give_b(jnp.int32(NZ - 1))
    group(NZ - 1)
    give_a(jnp.int32(NZ * NX - 2))
    give_a(jnp.int32(NZ * NX - 1))

    units = NZ * NX + NZ
    wait(qv.at[pl.ds(0, units - 2)], r_o)
    wait(qv.at[pl.ds(0, 2)], l_o)
    wait(qv.at[pl.ds(0, units - 2)], s_o)
    wait(qv.at[pl.ds(0, units - 2)], s_q)
    wait(meta_v.at[pl.ds(0, NZ - 1)], s_m)
    wait(kva.at[pl.ds(0, units - 2)], s_1)
    wait(kva.at[pl.ds(0, sent["a"])], s_a)
    wait(kvb.at[pl.ds(0, sent["b"])], s_b)


def body(queries, keys, values, block_lists, block_counts):
    zz, rest = block_lists // (NY * NX * NC), block_lists % (NY * NX * NC)
    yy, rest = rest // (NX * NC), rest % (NX * NC)
    xx, cc = rest // NC, rest % NC
    slot_a = ((yy * NC + cc) * NZ + zz) * NX + xx
    slot_b = ((xx * NC + cc) * NY + yy) * NZ + zz
    rows = NX * NC
    meta = (
        jnp.pad(slot_a, ((0, rows), (0, 128 - LIST_LEN)))
        + jnp.pad(slot_b, ((0, rows), (SLOT_B_LANE, 128 - LIST_LEN - SLOT_B_LANE)))
        + jnp.pad(block_counts[None, :], ((rows, rows - 1), (0, 128 - rows)))
    )
    dma = pltpu.SemaphoreType.DMA
    units = NZ * NX + NZ
    return pl.pallas_call(
        kernel,
        out_shape=jax.ShapeDtypeStruct(queries.shape, jnp.bfloat16),
        in_specs=[pl.BlockSpec(memory_space=pl.ANY)] * 4,
        out_specs=pl.BlockSpec(memory_space=pl.ANY),
        scratch_shapes=[
            pltpu.VMEM((NBLOCKS, 2, BL, HD), jnp.bfloat16),
            pltpu.VMEM((NBLOCKS, 2, BL, HD), jnp.bfloat16),
            pltpu.VMEM((units, BL, HD), jnp.bfloat16),
            pltpu.VMEM((units, BL, HD), jnp.bfloat16),
            pltpu.VMEM((NZ, 2 * NX * NC, 128), jnp.int32),
            pltpu.SMEM((NZ, 2 * NX * NC, 128), jnp.int32),
            pltpu.VMEM((2, LIST_LEN // 2, BL, 2 * BL), jnp.float32),
            dma((2,)), dma((2,)), dma, dma, dma,
            dma, dma, dma, dma, dma, dma,
            dma((NZ,)), dma((NZ,)), dma((NZ,)), dma, dma, dma,
            dma((2, NZ)), dma((NZ,)), dma,
            dma((2,)), dma((2,)), dma, dma((2, 3)), dma((2, 2)), dma((2, 4)),
            dma((2,)), dma((2,)), dma((2, 4)), dma((2, 4)),
        ],
        compiler_params=pltpu.CompilerParams(collective_id=0, has_side_effects=True, vmem_limit_bytes=52 << 20),
    )(queries, keys, values, meta)


def solution(mesh):
    placed = (
        P(("seq", "uly"), None),
        P(("seq", "uly"), None),
        P(("seq", "uly"), None),
        P("seq", None),
        P("seq"),
    )
    return jax.shard_map(
        body, mesh=mesh, in_specs=placed, out_specs=P(("seq", "uly"), None), check_vma=False
    )
```
